512 devices in a mesh: row: 32 (over x_lo, z), col: 16 (over x_hi, y, core).
Axes of the slice: x: 4 (x_hi: 2, x_lo: 2; x = x_hi * 2 + x_lo), y: 4, z: 16, core: 2. Of those that a mesh axis runs over, the one named last changes fastest.
Arguments:
- elemental: bfloat16 [2, 512, 512, 512], P(None, 'row', 'col'), may hold values from -6 to 6
- perambulators: bfloat16 [512, 2, 512, 512], P(('row', 'col')), may hold values from -0.1875 to 0.1875
- source_owner: int32 [1], replicated, may hold values from 0 to 511
Outputs:
- contracted: float32 [2, 512, 512, 512], P(None, None, 'row', 'col')
The draws below stay inside these ranges and needn't reach their ends.
All inputs are finite; a program needn't handle non-finite values.
Results may differ from the reference program's by a relative error of at most 0.0041.
Values may be sent and summed in bfloat16 or wider, within the bound.
A program may use at most 64 MiB of HBM per device.

```python
import jax
import jax.numpy as jnp

N = 512
SOURCES = 512


def shard_levels(key, dims, split, smallest, largest):
    loudness, own = 1.0, jax.random.fold_in(key, 6)
    for dim, shards_of in split:
        steps = jnp.exp(jax.random.uniform(jax.random.fold_in(own, dim), (shards_of,), jnp.float32, smallest / len(split), largest / len(split)))
        loudness = loudness * jnp.repeat(steps, dims[dim] // shards_of).reshape([-1 if axis == dim else 1 for axis in range(len(dims))])
    return loudness


def gaussian(rng, shape, scale, reach, shards=(), kind=jnp.bfloat16):
    drawn = jax.random.normal(rng, shape, jnp.float32) * scale
    if len(shards) > 0:
        drawn = shard_levels(rng, shape, shards, -0.22, 0.18) * drawn
    return jnp.clip(drawn, min=-reach, max=reach).astype(kind)


def setup_inputs(seed: int = 0) -> dict:
    streams_of = jax.random.split(jax.random.key(seed), 4)
    elemental = gaussian(streams_of[0], (2, N, N, N), 1.0, 6.0, ((1, 32), (2, 16)))
    perambulators = gaussian(streams_of[1], (SOURCES, 2, N, N), (2 * N) ** -0.5, 0.1875, ((0, 512),))
    source_owner = jax.random.randint(streams_of[2], (1,), 0, SOURCES).astype(jnp.int32)
    return {"elemental": elemental, "perambulators": perambulators, "source_owner": source_owner}


def build_mixing(peramb):
    real_part = peramb[0]
    imag_part = peramb[1]
    upper = jnp.concatenate([real_part, -imag_part], axis=1)
    lower = jnp.concatenate([imag_part, real_part], axis=1)
    full = jnp.concatenate([upper, lower], axis=0)
    return full.reshape(2, N, 2, N)


def reference(elemental, perambulators, source_owner):
    chosen = perambulators[source_owner[0]]
    mixing = build_mixing(chosen).astype(jnp.float32)
    first = jnp.einsum("scrk,rijk->sijc", mixing, elemental.astype(jnp.float32))
    first = first.astype(jnp.bfloat16).astype(jnp.float32)
    second = jnp.einsum("sbrj,rijc->sbic", mixing, first)
    second = second.astype(jnp.bfloat16).astype(jnp.float32)
    return jnp.einsum("sari,rbic->sabc", mixing, second)
```

```python
import functools

import jax
import jax.numpy as jnp
from jax import lax
from jax.experimental import pallas as pl
from jax.experimental.pallas import tpu as pltpu
from jax.sharding import PartitionSpec as P

MESH = pl.DeviceIdType.MESH
F32 = jnp.float32
BF16 = jnp.bfloat16
NT = (((1,), (1,)), ((), ()))


def butterfly(arrs, group):
    arrs = list(arrs)
    lane = lax.broadcasted_iota(jnp.int32, arrs[0].shape, 1)
    bit = 1
    while bit < len(arrs):
        shift = group * bit
        high = (lane & shift) != 0
        for a in range(len(arrs)):
            if a & bit:
                continue
            lo, hi = arrs[a], arrs[a | bit]
            arrs[a] = jnp.where(high, pltpu.roll(hi, shift, 1), lo)
            arrs[a | bit] = jnp.where(high, hi, pltpu.roll(lo, 128 - shift, 1))
        bit *= 2
    return arrs


def kernel(
    own_ref, e_ref, p_ref, out_ref,
    pb, mine, half, rb, cbuf, zb, dbuf, zg, qbuf, pp, m2, m3, x1, y1, r1, x2, sb, r2, x3, acc,
    pair_s, pair_r, plane_s, plane_r, zgrp_s, zgrp_r, zall_s, zall_r, gath_s, gath_r, back_s, back_r,
    local_sem, load_sem, col_s, col_r, row_s, row_r, out_sem,
):
    row = lax.axis_index("row")
    col = lax.axis_index("col")
    x_lo, z = row // 16, row % 16
    core, xy = col % 2, col // 2
    chip = x_lo * 8 + xy
    member, zgroup = z % 4, z // 4

    def at_chip(c):
        return ((c // 8) * 16 + z, (c % 8) * 2 + core)

    load_own = pltpu.make_async_copy(p_ref.at[core], mine, local_sem)
    load_own.start()
    for r in range(2):
        pltpu.make_async_copy(e_ref.at[r], x1.at[:, pl.ds(r * 512, 512)], load_sem).start()

    barrier = pltpu.get_barrier_semaphore()

    def greet(dev):
        pl.semaphore_signal(barrier, inc=1, device_id=dev, device_id_type=MESH)

    def greet_plane(d, _):
        greet(at_chip((chip + d) % 16))
        return 0

    def greet_other(d, _):
        greet((row, d * 2 + 1 - core))
        return 0

    def greet_row(d, _):
        for x in range(2):
            greet((x * 16 + (z + d) % 16, col))
        return 0

    lax.fori_loop(1, 16, greet_row, 0)
    lax.fori_loop(1, 16, greet_plane, 0)
    lax.fori_loop(0, 8, greet_other, 0)
    pl.semaphore_wait(barrier, 53)

    def send(src, dst, ssem, rsem, dev):
        pltpu.make_async_remote_copy(
            src_ref=src, dst_ref=dst, send_sem=ssem, recv_sem=rsem,
            device_id=dev, device_id_type=MESH,
        ).start()

    def wait_bytes(ref, sem):
        pltpu.make_async_copy(ref, ref, sem).wait()

    send(p_ref.at[1 - core], pb, pair_s, pair_r, (row, xy * 2 + 1 - core))
    load_own.wait()
    wait_bytes(pb, pair_r)
    from_me = own_ref[0] == core

    def pick(n, _):
        rows = pl.ds(pl.multiple_of(n * 32, 32), 32)
        half[rows, :] = jnp.where(from_me, mine[rows, :].astype(F32), pb[rows, :].astype(F32)).astype(BF16)
        return 0

    lax.fori_loop(0, 16, pick, 0)

    def rows32(n):
        return pl.ds(pl.multiple_of(n * 32, 32), 32)

    def scatter_plane(d, _):
        c = (chip + d) % 16
        send(half.at[rows32(c), :], rb.at[chip], plane_s, plane_r, at_chip(c))
        return 0

    lax.fori_loop(1, 16, scatter_plane, 0)
    pltpu.make_async_copy(half.at[rows32(chip), :], rb.at[chip], plane_r).start()
    wait_bytes(rb, plane_r)
    cbuf[...] = rb[own_ref[1]]

    def lanes128(n):
        return pl.ds(pl.multiple_of(n * 128, 128), 128)

    def scatter_z(d, _):
        m = (member + d) % 4
        send(cbuf.at[:, lanes128(m)], zb.at[member], zgrp_s, zgrp_r, (x_lo * 16 + zgroup * 4 + m, col))
        return 0

    lax.fori_loop(1, 4, scatter_z, 0)
    pltpu.make_async_copy(cbuf.at[:, lanes128(member)], zb.at[member], zgrp_r).start()
    wait_bytes(zb, zgrp_r)
    dbuf[...] = zb[own_ref[2]]

    def gather_z(d, _):
        dz = 8 + jnp.where(d % 2 == 0, d // 2, -((d + 1) // 2))
        send(dbuf, zg.at[z], zall_s, zall_r, (x_lo * 16 + (z + dz) % 16, col))
        return 0

    lax.fori_loop(0, 15, gather_z, 0)
    pltpu.make_async_copy(dbuf, zg.at[z], zall_r).start()
    wait_bytes(zg, zall_r)
    for m in range(4):
        qbuf[:, m * 128 : (m + 1) * 128] = zg[own_ref[3] * 4 + m]

    def gather_plane(d, _):
        c = (chip + d) % 16
        send(qbuf, pp.at[core, rows32(chip), :], gath_s, gath_r.at[chip], at_chip(c))
        return 0

    lax.fori_loop(1, 16, gather_plane, 0)
    pltpu.make_async_copy(qbuf, pp.at[core, rows32(chip), :], gath_r.at[chip]).start()

    def gather_pair(d, _):
        c = (chip + d) % 16
        part = pp.at[core, rows32(c), :]
        wait_bytes(part, gath_r.at[c])
        send(part, part, back_s, back_r, (row, xy * 2 + 1 - core))
        return 0

    lax.fori_loop(0, 16, gather_pair, 0)
    wait_bytes(pb, back_r)

    def build(n, _):
        rows = rows32(n)
        low = pl.ds(pl.multiple_of(512 + n * 32, 32), 32)
        re, im = pp[0, rows, :], pp[1, rows, :]
        m2[rows, 0:512] = re
        m2[rows, 512:1024] = -im
        m2[low, 0:512] = im
        m2[low, 512:1024] = re
        return 0

    lax.fori_loop(0, 16, build, 0)
    wait_bytes(x1, load_sem)

    for h in range(2):
        def contract_k(n, _, h=h):
            rows = pl.ds(pl.multiple_of(n * 256, 256), 256)
            y = lax.dot_general(m2[rows, :], x1[h * 256 : (h + 1) * 256, :], NT, preferred_element_type=F32)
            y1[h, n // 2, pl.ds(pl.multiple_of((n % 2) * 256, 256), 256), :] = y.astype(BF16)
            return 0

        lax.fori_loop(0, 4, contract_k, 0)

        for ch in range(2):
            q = h * 2 + ch

            def part(c, h=h, ch=ch):
                return y1.at[h, :, pl.ds(pl.multiple_of(c * 32 + ch * 16, 16), 16), :]

            def scatter_col(d, _, q=q, part=part):
                c = (col + d) % 16
                send(part(c), r1.at[q, col], col_s.at[q], col_r.at[q], (row, c))
                return 0

            lax.fori_loop(1, 16, scatter_col, 0)
            pltpu.make_async_copy(part(col), r1.at[q, col], col_r.at[q]).start()

    def second_step(q, _):
        wait_bytes(r1.at[q], col_r.at[q])

        def swap_in(n, _):
            r, chi = n // 4, n % 4
            for ib in range(2):
                got = [r1[q, chi * 4 + k, r, :, ib * 128 : (ib + 1) * 128].astype(F32) for k in range(4)]
                for k, v in enumerate(butterfly(got, 32)):
                    x2[(ib * 4 + k) * 16 : (ib * 4 + k + 1) * 16, lanes128(n)] = v.astype(BF16)
            return 0

        lax.fori_loop(0, 8, swap_in, 0)

        def contract_j(n, _):
            rows = pl.ds(pl.multiple_of(n * 128, 128), 128)
            y = lax.dot_general(x2[...], m2[rows, :], NT, preferred_element_type=F32)
            s, hi = n // 4, n % 4
            got = [y[k * 16 : (k + 1) * 16, :] for k in range(8)]
            for k, v in enumerate(butterfly(got, 16)):
                sb[q, hi * 8 + k, s, :, :] = v.astype(BF16)
            return 0

        lax.fori_loop(0, 8, contract_j, 0)

        def scatter_row(d, _):
            dz = 8 + jnp.where(d % 2 == 0, d // 2, -((d + 1) // 2))
            for dx in range(2):
                to = ((x_lo + dx) % 2) * 16 + (z + dz) % 16
                send(sb.at[q, to], r2.at[q, row], row_s.at[q], row_r.at[q], (to, col))
            return 0

        lax.fori_loop(0, 15, scatter_row, 0)
        to = (1 - x_lo) * 16 + z
        send(sb.at[q, to], r2.at[q, row], row_s.at[q], row_r.at[q], (to, col))
        pltpu.make_async_copy(sb.at[q, row], r2.at[q, row], row_r.at[q]).start()
        return 0

    lax.fori_loop(0, 4, second_step, 0)

    a = lax.broadcasted_iota(jnp.int32, (256, 128), 0)
    b = lax.broadcasted_iota(jnp.int32, (256, 128), 1)
    for h in range(2):
        perm = (a == (b % 16) * 16 + h * 8 + b // 16).astype(F32).astype(BF16)

        def permute(n, _, h=h, perm=perm):
            rows = pl.ds(pl.multiple_of(n * 256, 256), 256)
            for k in range(4):
                v = jnp.dot(m2[rows, k * 256 : (k + 1) * 256], perm, preferred_element_type=F32)
                m3[h, rows, k * 128 : (k + 1) * 128] = v.astype(BF16)
            return 0

        lax.fori_loop(0, 4, permute, 0)

    def third_step(q, first):
        h, ch = q // 2, q % 2
        wait_bytes(r2.at[q], row_r.at[q])

        def swap_out(n, _):
            r, x = n // 2, n % 2
            got = [r2[q, x * 16 + k, r, :, :].astype(F32) for k in range(16)]
            for k, v in enumerate(butterfly(got, 1)):
                x3[k * 16 : (k + 1) * 16, lanes128(n)] = v.astype(BF16)
            return 0

        lax.fori_loop(0, 4, swap_out, 0)

        def contract_i(n, _):
            rows = pl.ds(pl.multiple_of(n * 256, 256), 256)
            s = n // 2
            lanes = pl.ds(pl.multiple_of((n % 2) * 256, 256), 256)
            y = lax.dot_general(x3[...], m3[h, rows, :], NT, preferred_element_type=F32)
            y = y.reshape(16, 16, 256)
            if first:
                acc[ch, s, :, :, lanes] = y
            else:
                acc[ch, s, :, :, lanes] += y
            return 0

        lax.fori_loop(0, 4, contract_i, 0)

    for q in range(2):
        third_step(q, True)
    for q in range(2, 4):
        third_step(q, False)
        ch = q % 2
        pltpu.make_async_copy(acc.at[ch], out_ref.at[:, :, pl.ds(ch * 16, 16), :], out_sem).start()

    wait_bytes(pb, pair_s)
    wait_bytes(rb.at[pl.ds(0, 15)], plane_s)
    wait_bytes(zb.at[pl.ds(0, 3)], zgrp_s)
    wait_bytes(zg.at[pl.ds(0, 15)], zall_s)
    wait_bytes(rb.at[pl.ds(0, 15)], gath_s)
    wait_bytes(pb, back_s)
    for q in range(4):
        wait_bytes(r1.at[q, pl.ds(0, 15)], col_s.at[q])
        wait_bytes(r2.at[q, pl.ds(0, 31)], row_s.at[q])
    wait_bytes(acc, out_sem)


def per_device(elemental, perambulators, source_owner):
    owner = source_owner[0]
    row, col = owner // 16, owner % 16
    own = jnp.stack([col % 2, (row // 16) * 8 + col // 2, row % 4, (row % 16) // 4]).astype(jnp.int32)
    dma = pltpu.SemaphoreType.DMA
    vmem = pltpu.VMEM
    out = pl.pallas_call(
        kernel,
        out_shape=jax.ShapeDtypeStruct((2, 16, 32, 512), F32),
        in_specs=[
            pl.BlockSpec(memory_space=pltpu.SMEM),
            pl.BlockSpec(memory_space=pl.ANY),
            pl.BlockSpec(memory_space=pl.ANY),
        ],
        out_specs=pl.BlockSpec(memory_space=pl.ANY),
        scratch_shapes=[
            vmem((512, 512), BF16),
            vmem((512, 512), BF16),
            vmem((512, 512), BF16),
            vmem((16, 32, 512), BF16),
            vmem((32, 512), BF16),
            vmem((4, 32, 128), BF16),
            vmem((32, 128), BF16),
            vmem((16, 32, 128), BF16),
            vmem((32, 512), BF16),
            vmem((2, 512, 512), BF16),
            vmem((1024, 1024), BF16),
            vmem((2, 1024, 512), BF16),
            vmem((512, 1024), BF16),
            vmem((2, 2, 512, 256), BF16),
            vmem((4, 16, 2, 16, 256), BF16),
            vmem((128, 1024), BF16),
            vmem((4, 32, 2, 16, 128), BF16),
            vmem((4, 32, 2, 16, 128), BF16),
            vmem((256, 512), BF16),
            vmem((2, 2, 16, 16, 512), F32),
            dma, dma, dma, dma, dma, dma, dma, dma, dma, dma((16,)), dma, dma,
            dma, dma, dma((4,)), dma((4,)), dma((4,)), dma((4,)), dma,
        ],
        compiler_params=pltpu.CompilerParams(collective_id=0, has_side_effects=True),
    )(own, elemental.reshape(2, 512, 512), perambulators[0])
    return out.transpose(0, 3, 1, 2)


def solution(mesh):
    in_specs = (P(None, "row", "col", None), P(("row", "col"), None, None, None), P())
    out_specs = P(None, None, "row", "col")
    return jax.shard_map(
        per_device, mesh=mesh, in_specs=in_specs, out_specs=out_specs, check_vma=False
    )
```

```python
import functools

import jax
import jax.numpy as jnp
from jax import lax
from jax.experimental import pallas as pl
from jax.experimental.pallas import tpu as pltpu
from jax.sharding import PartitionSpec as P

MESH = pl.DeviceIdType.MESH
F32 = jnp.float32
BF16 = jnp.bfloat16
NT = (((1,), (1,)), ((), ()))
FAR_FIRST = sorted(
    ((dx, dy) for dx in range(4) for dy in range(4) if dx or dy),
    key=lambda d: -(min(d[0], 4 - d[0]) + min(d[1], 4 - d[1])),
)


def butterfly(arrs, group):
    arrs = list(arrs)
    lane = lax.broadcasted_iota(jnp.int32, arrs[0].shape, 1)
    bit = 1
    while bit < len(arrs):
        shift = group * bit
        high = (lane & shift) != 0
        for a in range(len(arrs)):
            if a & bit:
                continue
            lo, hi = arrs[a], arrs[a | bit]
            arrs[a] = jnp.where(high, pltpu.roll(hi, shift, 1), lo)
            arrs[a | bit] = jnp.where(high, hi, pltpu.roll(lo, 128 - shift, 1))
        bit *= 2
    return arrs


def kernel(
    own_ref, e_ref, p_ref, acc, x3, m3b,
    pb, mine, half, rb, cbuf, zb, dbuf, zg, qbuf, pp, m2, m3a, x1, y1, r1, x2, sb, r2,
    pair_s, pair_r, plane_s, plane_r, zgrp_s, zgrp_r, zall_s, zall_r, gath_s, gath_r, back_s, back_r,
    local_sem, load_sem, col_s, col_r, row_s, row_r,
):
    row = lax.axis_index("row")
    col = lax.axis_index("col")
    x_lo, z = row // 16, row % 16
    core, xy = col % 2, col // 2
    chip = x_lo * 8 + xy
    member, zgroup = z % 4, z // 4
    zhalf, zrest = z // 8, z % 8
    x_hi, y = xy // 4, xy % 4
    x = x_hi * 2 + x_lo
    other = (row, xy * 2 + 1 - core)

    def in_plane(dx, dy):
        px, py = (x + dx) % 4, (y + dy) % 4
        to = (px // 2) * 4 + py
        return (px % 2) * 8 + to, ((px % 2) * 16 + z, to * 2 + core)

    barrier = pltpu.get_barrier_semaphore()

    def greet(dev):
        pl.semaphore_signal(barrier, inc=1, device_id=dev, device_id_type=MESH)

    def greet_other(d, _):
        greet((row, d * 2 + 1 - core))
        return 0

    def greet_row(d, _):
        for x in range(2):
            greet((x * 16 + (z + d) % 16, col))
        return 0

    lax.fori_loop(1, 16, greet_row, 0)
    for step in FAR_FIRST:
        greet(in_plane(*step)[1])
    lax.fori_loop(0, 8, greet_other, 0)

    load_own = pltpu.make_async_copy(p_ref.at[core], mine, local_sem)
    load_own.start()
    for r in range(2):
        pltpu.make_async_copy(e_ref.at[r], x1.at[:, pl.ds(r * 512, 512)], load_sem).start()
    pl.semaphore_wait(barrier, 53)

    def send(src, dst, ssem, rsem, dev):
        pltpu.make_async_remote_copy(
            src_ref=src, dst_ref=dst, send_sem=ssem, recv_sem=rsem,
            device_id=dev, device_id_type=MESH,
        ).start()

    def wait_bytes(ref, sem):
        pltpu.make_async_copy(ref, ref, sem).wait()

    send(p_ref.at[1 - core], pb, pair_s, pair_r, other)
    load_own.wait()
    wait_bytes(pb, pair_r)
    owner = own_ref[0]
    owner_row, owner_col = lax.div(owner, 16), lax.rem(owner, 16)
    from_me = lax.rem(owner_col, 2) == core
    owner_chip = lax.div(owner_row, 16) * 8 + lax.div(owner_col, 2)
    owner_z = lax.rem(owner_row, 16)

    def pick(n, _):
        rows = pl.ds(pl.multiple_of(n * 32, 32), 32)
        half[rows, :] = jnp.where(from_me, mine[rows, :], pb[rows, :])
        return 0

    lax.fori_loop(0, 16, pick, 0)

    def rows32(n):
        return pl.ds(pl.multiple_of(n * 32, 32), 32)

    for step in FAR_FIRST:
        c, to = in_plane(*step)
        send(half.at[rows32(c), :], rb.at[chip], plane_s, plane_r, to)
    pltpu.make_async_copy(half.at[rows32(chip), :], rb.at[chip], plane_r).start()
    wait_bytes(rb, plane_r)
    cbuf[...] = rb[owner_chip]

    def lanes128(n):
        return pl.ds(pl.multiple_of(n * 128, 128), 128)

    def scatter_z(d, _):
        m = (member + d) % 4
        send(cbuf.at[:, lanes128(m)], zb.at[member], zgrp_s, zgrp_r, (x_lo * 16 + zgroup * 4 + m, col))
        return 0

    lax.fori_loop(1, 4, scatter_z, 0)
    pltpu.make_async_copy(cbuf.at[:, lanes128(member)], zb.at[member], zgrp_r).start()
    wait_bytes(zb, zgrp_r)
    dbuf[...] = zb[lax.rem(owner_z, 4)]

    def gather_z(d, _):
        dz = 8 + jnp.where(d % 2 == 0, d // 2, -((d + 1) // 2))
        send(dbuf, zg.at[z], zall_s, zall_r, (x_lo * 16 + (z + dz) % 16, col))
        return 0

    lax.fori_loop(0, 15, gather_z, 0)
    pltpu.make_async_copy(dbuf, zg.at[z], zall_r).start()
    wait_bytes(zg, zall_r)
    for m in range(4):
        qbuf[:, m * 128 : (m + 1) * 128] = zg[lax.div(owner_z, 4) * 4 + m]

    for step in FAR_FIRST:
        send(qbuf, pp.at[core, rows32(chip), :], gath_s, gath_r.at[chip], in_plane(*step)[1])
    pltpu.make_async_copy(qbuf, pp.at[core, rows32(chip), :], gath_r.at[chip]).start()
    for step in ((0, 0), *FAR_FIRST):
        c = in_plane(*step)[0]
        part = pp.at[core, rows32(c), :]
        wait_bytes(part, gath_r.at[c])
        send(part, part, back_s, back_r, other)
    wait_bytes(pb, back_r)

    def build(n, _):
        re, im = pp[0, rows32(n), :].reshape(2, 16, 512), pp[1, rows32(n), :].reshape(2, 16, 512)
        m2[0, n, :, :, 0:512] = re
        m2[0, n, :, :, 512:1024] = -im
        m2[1, n, :, :, 0:512] = im
        m2[1, n, :, :, 512:1024] = re
        return 0

    lax.fori_loop(0, 16, build, 0)
    wait_bytes(x1, load_sem)

    def contract_k(q):
        h, ch = q // 2, q % 2
        for s in range(2):
            y = lax.dot_general(
                m2[s, :, ch].reshape(256, 1024), x1[h * 256 : (h + 1) * 256, :], NT, preferred_element_type=F32
            )
            y1[q, s] = y.astype(BF16)

    def exchange_col(q):
        def scatter_col(n, _):
            k = n % 8
            dy = jnp.where(k // 2 == 0, 2, jnp.where(k // 2 == 1, 1, jnp.where(k // 2 == 2, 3, 0)))
            c = (((x_hi + 1 - n // 8) % 2) * 4 + (y + dy) % 4) * 2 + (core + 1 - k % 2) % 2
            rows = pl.ds(pl.multiple_of(c * 16, 16), 16)
            send(y1.at[q, :, rows, :], r1.at[q, col], col_s.at[q], col_r.at[q, col // 4], (row, c))
            return 0

        lax.fori_loop(0, 15, scatter_col, 0)
        rows = pl.ds(pl.multiple_of(col * 16, 16), 16)
        pltpu.make_async_copy(y1.at[q, :, rows, :], r1.at[q, col], col_r.at[q, col // 4]).start()

    def contract_j(q):
        def swap_in(n, _):
            chi = (col // 4 + n) % 4
            wait_bytes(r1.at[q, pl.ds(chi * 4, 4)], col_r.at[q, chi])
            for r in range(2):
                for ib in range(2):
                    got = [r1[q, chi * 4 + k, r, :, ib * 128 : (ib + 1) * 128] for k in range(4)]
                    for k, v in enumerate(butterfly(got, 32)):
                        x2[(ib * 4 + k) * 16 : (ib * 4 + k + 1) * 16, lanes128(r * 4 + chi)] = v
            return 0

        lax.fori_loop(0, 4, swap_in, 0)

        for dx, dz in ((1, 1), (0, 1), (1, 0), (0, 0)):
            to_x, to_half = (x_lo + dx) % 2, (zhalf + dz) % 2
            hi = to_x * 2 + to_half
            y = lax.dot_general(
                x2[...], m2[:, pl.ds(hi * 4, 4)].reshape(256, 1024), NT, preferred_element_type=F32
            ).astype(BF16)
            for s in range(2):
                got = [y[k * 16 : (k + 1) * 16, s * 128 : (s + 1) * 128] for k in range(8)]
                for k, v in enumerate(butterfly(got, 16)):
                    sb[q, hi * 8 + k, s, :, :] = v

            def scatter_row(d, _):
                to = to_x * 16 + to_half * 8 + (zrest + d) % 8
                send(sb.at[q, to], r2.at[q, row], row_s.at[q], row_r.at[q], (to, col))
                return 0

            lax.fori_loop(0 if dx or dz else 1, 8, scatter_row, 0)
        pltpu.make_async_copy(sb.at[q, row], r2.at[q, row], row_r.at[q]).start()

    contract_k(0)
    exchange_col(0)
    for q in (1, 2, 3):
        contract_k(q)
    exchange_col(1)
    contract_j(0)
    exchange_col(2)
    contract_j(1)
    exchange_col(3)
    contract_j(2)
    contract_j(3)

    a = lax.broadcasted_iota(jnp.int32, (256, 128), 0)
    b = lax.broadcasted_iota(jnp.int32, (256, 128), 1)
    for h in range(2):
        perm = (a == (b % 16) * 16 + h * 8 + b // 16).astype(F32).astype(BF16)

        m3 = (m3a, m3b)[h]

        def permute(n, _, m3=m3, perm=perm):
            block = m2[n // 2, pl.ds((n % 2) * 8, 8)].reshape(256, 1024)
            rows = pl.ds(pl.multiple_of(n * 256, 256), 256)
            for k in range(4):
                v = jnp.dot(block[:, k * 256 : (k + 1) * 256], perm, preferred_element_type=F32)
                m3[rows, k * 128 : (k + 1) * 128] = v.astype(BF16)
            return 0

        lax.fori_loop(0, 4, permute, 0)

    for q in range(4):
        ch = q % 2
        wait_bytes(r2.at[q], row_r.at[q])

        def swap_out(n, _, q=q):
            r, x = n // 2, n % 2
            got = [r2[q, x * 16 + k, r, :, :] for k in range(16)]
            for k, v in enumerate(butterfly(got, 1)):
                x3[k * 16 : (k + 1) * 16, lanes128(n)] = v
            return 0

        lax.fori_loop(0, 4, swap_out, 0)
        if q == 3:
            break
        m3 = (m3a, m3b)[q // 2]

        def contract_i(n, _, q=q, ch=ch, m3=m3):
            rows = pl.ds(pl.multiple_of(n * 256, 256), 256)
            lanes = pl.ds(pl.multiple_of((n % 2) * 256, 256), 256)
            v = lax.dot_general(x3[...], m3[rows, :], NT, preferred_element_type=F32).reshape(16, 16, 256)
            if q < 2:
                acc[ch, n // 2, :, :, lanes] = v
            else:
                acc[ch, n // 2, :, :, lanes] += v
            return 0

        lax.fori_loop(0, 4, contract_i, 0)

    wait_bytes(pb, pair_s)
    wait_bytes(rb.at[pl.ds(0, 15)], plane_s)
    wait_bytes(zb.at[pl.ds(0, 3)], zgrp_s)
    wait_bytes(zg.at[pl.ds(0, 15)], zall_s)
    wait_bytes(rb.at[pl.ds(0, 15)], gath_s)
    wait_bytes(pb, back_s)
    for q in range(4):
        wait_bytes(r1.at[q, pl.ds(0, 15)], col_s.at[q])
        wait_bytes(r2.at[q, pl.ds(0, 31)], row_s.at[q])


def finish(acc, x3, m3, out_ref, last, sem):
    done = pltpu.make_async_copy(acc.at[0], out_ref.at[:, :, pl.ds(0, 16), :], sem.at[2])
    done.start()
    copies = []
    for s in range(2):
        for lane in range(0, 512, 256):
            v = lax.dot_general(
                x3[...], m3[s * 512 + lane : s * 512 + lane + 256, :], NT, preferred_element_type=F32
            )
            last[s, :, :, lane : lane + 256] = acc[1, s, :, :, lane : lane + 256] + v.reshape(16, 16, 256)
        copies.append(pltpu.make_async_copy(last.at[s], out_ref.at[s, :, pl.ds(16, 16), :], sem.at[s]))
        copies[-1].start()
    for copy in (done, *copies):
        copy.wait()


def per_device(elemental, perambulators, source_owner):
    dma = pltpu.SemaphoreType.DMA
    vmem = pltpu.VMEM
    held = pl.BlockSpec(memory_space=pltpu.VMEM)
    parts = pl.pallas_call(
        kernel,
        out_shape=(vmem((2, 2, 16, 16, 512), F32), vmem((256, 512), BF16), vmem((1024, 512), BF16)),
        in_specs=[
            pl.BlockSpec(memory_space=pltpu.SMEM),
            pl.BlockSpec(memory_space=pltpu.HBM),
            pl.BlockSpec(memory_space=pltpu.HBM),
        ],
        out_specs=(held, held, held),
        scratch_shapes=[
            vmem((512, 512), BF16),
            vmem((512, 512), BF16),
            vmem((512, 512), BF16),
            vmem((16, 32, 512), BF16),
            vmem((32, 512), BF16),
            vmem((4, 32, 128), BF16),
            vmem((32, 128), BF16),
            vmem((16, 32, 128), BF16),
            vmem((32, 512), BF16),
            vmem((2, 512, 512), BF16),
            vmem((2, 16, 2, 16, 1024), BF16),
            vmem((1024, 512), BF16),
            vmem((512, 1024), BF16),
            vmem((4, 2, 256, 256), BF16),
            vmem((4, 16, 2, 16, 256), BF16),
            vmem((128, 1024), BF16),
            vmem((4, 32, 2, 16, 128), BF16),
            vmem((4, 32, 2, 16, 128), BF16),
            dma, dma, dma, dma, dma, dma, dma, dma, dma, dma((16,)), dma, dma,
            dma, dma, dma((4,)), dma((4, 4)), dma((4,)), dma((4,)),
        ],
        compiler_params=pltpu.CompilerParams(collective_id=0, has_side_effects=True, vmem_limit_bytes=60 << 20),
    )(source_owner, elemental.reshape(2, 512, 512), perambulators[0])
    out = pl.pallas_call(
        finish,
        out_shape=jax.ShapeDtypeStruct((2, 16, 32, 512), F32),
        in_specs=[held, held, held],
        out_specs=pl.BlockSpec(memory_space=pltpu.HBM),
        scratch_shapes=[vmem((2, 16, 16, 512), F32), dma((3,))],
        compiler_params=pltpu.CompilerParams(vmem_limit_bytes=12 << 20),
    )(*parts)
    return out.transpose(0, 3, 1, 2)


def solution(mesh):
    in_specs = (P(None, "row", "col", None), P(("row", "col"), None, None, None), P())
    out_specs = P(None, None, "row", "col")
    return jax.shard_map(
        per_device, mesh=mesh, in_specs=in_specs, out_specs=out_specs, check_vma=False
    )
```

```python
import functools

import jax
import jax.numpy as jnp
from jax import lax
from jax.experimental import pallas as pl
from jax.experimental.pallas import tpu as pltpu
from jax.sharding import PartitionSpec as P

MESH = pl.DeviceIdType.MESH
F32 = jnp.float32
BF16 = jnp.bfloat16
NT = (((1,), (1,)), ((), ()))
FAR_FIRST = sorted(
    ((dx, dy) for dx in range(4) for dy in range(4) if dx or dy),
    key=lambda d: -(min(d[0], 4 - d[0]) + min(d[1], 4 - d[1])),
)


def butterfly(arrs, group):
    arrs = list(arrs)
    lane = lax.broadcasted_iota(jnp.int32, arrs[0].shape, 1)
    bit = 1
    while bit < len(arrs):
        shift = group * bit
        high = (lane & shift) != 0
        for a in range(len(arrs)):
            if a & bit:
                continue
            lo, hi = arrs[a], arrs[a | bit]
            arrs[a] = jnp.where(high, pltpu.roll(hi, shift, 1), lo)
            arrs[a | bit] = jnp.where(high, hi, pltpu.roll(lo, 128 - shift, 1))
        bit *= 2
    return arrs


def kernel(
    own_ref, e_ref, p_ref, acc, x3, m3b,
    pb, mine, half, rb0, rb1, cbuf, zb0, zb1, dbuf, zg0, zg1, qbuf, pp, m2, m3a, x1, y1, r1, x2, sb, r2,
    pair_s, pair_r, plane_s, plane_r, zgrp_s, zgrp_r, zall_s, zall_r, gath_s, gath_r, back_s, back_r,
    local_sem, load_sem, col_s, col_r, row_s, row_r,
):
    row = lax.axis_index("row")
    col = lax.axis_index("col")
    x_lo, z = row // 16, row % 16
    core, xy = col % 2, col // 2
    chip = x_lo * 8 + xy
    member, zgroup = z % 4, z // 4
    zhalf, zrest = z // 8, z % 8
    x_hi, y = xy // 4, xy % 4
    rb, zb, zg = (rb0, rb1), (zb0, zb1), (zg0, zg1)
    x = x_hi * 2 + x_lo
    other = (row, xy * 2 + 1 - core)

    def in_plane(dx, dy):
        px, py = (x + dx) % 4, (y + dy) % 4
        to = (px // 2) * 4 + py
        return (px % 2) * 8 + to, ((px % 2) * 16 + z, to * 2 + core)

    barrier = pltpu.get_barrier_semaphore()

    def greet(dev):
        pl.semaphore_signal(barrier, inc=1, device_id=dev, device_id_type=MESH)

    def greet_other(d, _):
        greet((row, d * 2 + 1 - core))
        return 0

    def greet_row(d, _):
        for x in range(2):
            greet((x * 16 + (z + d) % 16, col))
        return 0

    lax.fori_loop(1, 16, greet_row, 0)
    for step in FAR_FIRST:
        greet(in_plane(*step)[1])
    lax.fori_loop(0, 8, greet_other, 0)

    for t in range(2):
        pltpu.make_async_copy(p_ref.at[core, :, t], mine.at[t], local_sem.at[t]).start()
    for r in range(2):
        pltpu.make_async_copy(e_ref.at[r], x1.at[:, pl.ds(r * 512, 512)], load_sem).start()
    pl.semaphore_wait(barrier, 53)

    def send(src, dst, ssem, rsem, dev):
        pltpu.make_async_remote_copy(
            src_ref=src, dst_ref=dst, send_sem=ssem, recv_sem=rsem,
            device_id=dev, device_id_type=MESH,
        ).start()

    def wait_bytes(ref, sem):
        pltpu.make_async_copy(ref, ref, sem).wait()

    owner = own_ref[0]
    owner_row, owner_col = lax.div(owner, 16), lax.rem(owner, 16)
    from_me = lax.rem(owner_col, 2) == core
    owner_chip = lax.div(owner_row, 16) * 8 + lax.div(owner_col, 2)
    owner_z = lax.rem(owner_row, 16)

    def lanes128(n):
        return pl.ds(pl.multiple_of(n * 128, 128), 128)

    for t in range(2):
        send(p_ref.at[1 - core, :, t], pb.at[t], pair_s, pair_r.at[t], other)

    for t in range(2):
        wait_bytes(mine.at[t], local_sem.at[t])
        wait_bytes(pb.at[t], pair_r.at[t])

        def pick(n, _, t=t):
            half[t, n] = jnp.where(from_me, mine[t, n], pb[t, n])
            return 0

        lax.fori_loop(0, 16, pick, 0)
        for step in FAR_FIRST:
            c, to = in_plane(*step)
            send(half.at[t, c], rb[t].at[chip], plane_s.at[t], plane_r.at[t], to)
        pltpu.make_async_copy(half.at[t, chip], rb[t].at[chip], plane_r.at[t]).start()

    for t in range(2):
        wait_bytes(rb[t], plane_r.at[t])
        cbuf[t] = rb[t][owner_chip]

        def scatter_z(d, _, t=t):
            to = (x_lo * 16 + zgroup * 4 + (member + d) % 4, col)
            send(cbuf.at[t, :, lanes128((member + d) % 4)], zb[t].at[member], zgrp_s.at[t], zgrp_r.at[t], to)
            return 0

        lax.fori_loop(1, 4, scatter_z, 0)
        pltpu.make_async_copy(cbuf.at[t, :, lanes128(member)], zb[t].at[member], zgrp_r.at[t]).start()
    for t in range(2):
        wait_bytes(zb[t], zgrp_r.at[t])
        dbuf[t] = zb[t][lax.rem(owner_z, 4)]

        def gather_z(d, _, t=t):
            dz = 8 + jnp.where(d % 2 == 0, d // 2, -((d + 1) // 2))
            send(dbuf.at[t], zg[t].at[z], zall_s.at[t], zall_r.at[t], (x_lo * 16 + (z + dz) % 16, col))
            return 0

        lax.fori_loop(0, 15, gather_z, 0)
        pltpu.make_async_copy(dbuf.at[t], zg[t].at[z], zall_r.at[t]).start()

    for t in range(2):
        wait_bytes(zg[t], zall_r.at[t])
        for m in range(4):
            qbuf[t, :, m * 128 : (m + 1) * 128] = zg[t][lax.div(owner_z, 4) * 4 + m]
        for step in FAR_FIRST:
            send(qbuf.at[t], pp.at[core, t, chip], gath_s.at[t], gath_r.at[t, chip], in_plane(*step)[1])
        pltpu.make_async_copy(qbuf.at[t], pp.at[core, t, chip], gath_r.at[t, chip]).start()

    def gather_pair(t):
        for step in ((0, 0), *FAR_FIRST):
            c = in_plane(*step)[0]
            part = pp.at[core, t, c]
            wait_bytes(part, gath_r.at[t, c])
            send(part, part, back_s, back_r.at[t], other)
        wait_bytes(pb.at[t], back_r.at[t])

        def build(n, _):
            re, im = pp[0, t, n], pp[1, t, n]
            m2[0, n, t, :, 0:512] = re
            m2[0, n, t, :, 512:1024] = -im
            m2[1, n, t, :, 0:512] = im
            m2[1, n, t, :, 512:1024] = re
            return 0

        lax.fori_loop(0, 16, build, 0)

    def contract_k(q):
        h, ch = q // 2, q % 2
        for s in range(2):
            y = lax.dot_general(
                m2[s, :, ch].reshape(256, 1024), x1[h * 256 : (h + 1) * 256, :], NT, preferred_element_type=F32
            )
            y1[q, s] = y.astype(BF16)

    def exchange_col(q):
        def scatter_col(n, _):
            k = n % 8
            dy = jnp.where(k // 2 == 0, 2, jnp.where(k // 2 == 1, 1, jnp.where(k // 2 == 2, 3, 0)))
            c = (((x_hi + 1 - n // 8) % 2) * 4 + (y + dy) % 4) * 2 + (core + 1 - k % 2) % 2
            rows = pl.ds(pl.multiple_of(c * 16, 16), 16)
            send(y1.at[q, :, rows, :], r1.at[q, col], col_s.at[q], col_r.at[q, col // 4], (row, c))
            return 0

        lax.fori_loop(0, 15, scatter_col, 0)
        rows = pl.ds(pl.multiple_of(col * 16, 16), 16)
        pltpu.make_async_copy(y1.at[q, :, rows, :], r1.at[q, col], col_r.at[q, col // 4]).start()

    def contract_j(q):
        def swap_in(n, _):
            chi = (col // 4 + n) % 4
            wait_bytes(r1.at[q, pl.ds(chi * 4, 4)], col_r.at[q, chi])
            for r in range(2):
                for ib in range(2):
                    got = [r1[q, chi * 4 + k, r, :, ib * 128 : (ib + 1) * 128] for k in range(4)]
                    for k, v in enumerate(butterfly(got, 32)):
                        x2[(ib * 4 + k) * 16 : (ib * 4 + k + 1) * 16, lanes128(r * 4 + chi)] = v
            return 0

        lax.fori_loop(0, 4, swap_in, 0)

        for dx, dz in ((0, 1), (1, 1), (1, 0), (0, 0)):
            to_x, to_half = (x_lo + dx) % 2, (zhalf + dz) % 2
            hi = to_x * 2 + to_half
            y = lax.dot_general(
                x2[...], m2[:, pl.ds(hi * 4, 4)].reshape(256, 1024), NT, preferred_element_type=F32
            ).astype(BF16)
            for s in range(2):
                got = [y[k * 16 : (k + 1) * 16, s * 128 : (s + 1) * 128] for k in range(8)]
                for k, v in enumerate(butterfly(got, 16)):
                    sb[q, hi * 8 + k, s, :, :] = v

            def scatter_row(d, _):
                to = to_x * 16 + to_half * 8 + (zrest + d) % 8
                send(sb.at[q, to], r2.at[q, row], row_s.at[q], row_r.at[q], (to, col))
                return 0

            lax.fori_loop(0 if dx or dz else 1, 8, scatter_row, 0)
        pltpu.make_async_copy(sb.at[q, row], r2.at[q, row], row_r.at[q]).start()

    gather_pair(0)
    wait_bytes(x1, load_sem)
    contract_k(0)
    exchange_col(0)
    gather_pair(1)
    contract_k(1)
    exchange_col(1)
    contract_k(2)
    contract_k(3)
    contract_j(0)
    exchange_col(2)
    contract_j(1)
    exchange_col(3)
    contract_j(2)
    contract_j(3)

    a = lax.broadcasted_iota(jnp.int32, (256, 128), 0)
    b = lax.broadcasted_iota(jnp.int32, (256, 128), 1)
    for h in range(2):
        perm = (a == (b % 16) * 16 + h * 8 + b // 16).astype(F32).astype(BF16)

        m3 = (m3a, m3b)[h]

        def permute(n, _, m3=m3, perm=perm):
            block = m2[n // 2, pl.ds((n % 2) * 8, 8)].reshape(256, 1024)
            rows = pl.ds(pl.multiple_of(n * 256, 256), 256)
            for k in range(4):
                v = jnp.dot(block[:, k * 256 : (k + 1) * 256], perm, preferred_element_type=F32)
                m3[rows, k * 128 : (k + 1) * 128] = v.astype(BF16)
            return 0

        lax.fori_loop(0, 4, permute, 0)

    for q in range(4):
        ch = q % 2
        wait_bytes(r2.at[q], row_r.at[q])

        def swap_out(n, _, q=q):
            r, x = n // 2, n % 2
            got = [r2[q, x * 16 + k, r, :, :] for k in range(16)]
            for k, v in enumerate(butterfly(got, 1)):
                x3[k * 16 : (k + 1) * 16, lanes128(n)] = v
            return 0

        lax.fori_loop(0, 4, swap_out, 0)
        if q == 3:
            break
        m3 = (m3a, m3b)[q // 2]

        def contract_i(n, _, q=q, ch=ch, m3=m3):
            rows = pl.ds(pl.multiple_of(n * 256, 256), 256)
            lanes = pl.ds(pl.multiple_of((n % 2) * 256, 256), 256)
            v = lax.dot_general(x3[...], m3[rows, :], NT, preferred_element_type=F32).reshape(16, 16, 256)
            if q < 2:
                acc[ch, n // 2, :, :, lanes] = v
            else:
                acc[ch, n // 2, :, :, lanes] += v
            return 0

        lax.fori_loop(0, 4, contract_i, 0)

    wait_bytes(pb, pair_s)
    wait_bytes(pb, back_s)
    for t in range(2):
        wait_bytes(rb[t].at[pl.ds(0, 15)], plane_s.at[t])
        wait_bytes(zb[t].at[pl.ds(0, 3)], zgrp_s.at[t])
        wait_bytes(zg[t].at[pl.ds(0, 15)], zall_s.at[t])
        wait_bytes(rb[t].at[pl.ds(0, 15)], gath_s.at[t])
    for q in range(4):
        wait_bytes(r1.at[q, pl.ds(0, 15)], col_s.at[q])
        wait_bytes(r2.at[q, pl.ds(0, 31)], row_s.at[q])


def finish(acc, x3, m3, out_ref, last, sem):
    done = pltpu.make_async_copy(acc.at[0], out_ref.at[:, :, pl.ds(0, 16), :], sem.at[2])
    done.start()
    copies = []
    for s in range(2):
        for lane in range(0, 512, 256):
            v = lax.dot_general(
                x3[...], m3[s * 512 + lane : s * 512 + lane + 256, :], NT, preferred_element_type=F32
            )
            last[s, :, :, lane : lane + 256] = acc[1, s, :, :, lane : lane + 256] + v.reshape(16, 16, 256)
        copies.append(pltpu.make_async_copy(last.at[s], out_ref.at[s, :, pl.ds(16, 16), :], sem.at[s]))
        copies[-1].start()
    for copy in (done, *copies):
        copy.wait()


def per_device(elemental, perambulators, source_owner):
    dma = pltpu.SemaphoreType.DMA
    vmem = pltpu.VMEM
    held = pl.BlockSpec(memory_space=pltpu.VMEM)
    parts = pl.pallas_call(
        kernel,
        out_shape=(vmem((2, 2, 16, 16, 512), F32), vmem((256, 512), BF16), vmem((1024, 512), BF16)),
        in_specs=[
            pl.BlockSpec(memory_space=pltpu.SMEM),
            pl.BlockSpec(memory_space=pltpu.HBM),
            pl.BlockSpec(memory_space=pltpu.HBM),
        ],
        out_specs=(held, held, held),
        scratch_shapes=[
            vmem((2, 16, 16, 512), BF16),
            vmem((2, 16, 16, 512), BF16),
            vmem((2, 16, 16, 512), BF16),
            vmem((16, 16, 512), BF16),
            vmem((16, 16, 512), BF16),
            vmem((2, 16, 512), BF16),
            vmem((4, 16, 128), BF16),
            vmem((4, 16, 128), BF16),
            vmem((2, 16, 128), BF16),
            vmem((16, 16, 128), BF16),
            vmem((16, 16, 128), BF16),
            vmem((2, 16, 512), BF16),
            vmem((2, 2, 16, 16, 512), BF16),
            vmem((2, 16, 2, 16, 1024), BF16),
            vmem((1024, 512), BF16),
            vmem((512, 1024), BF16),
            vmem((4, 2, 256, 256), BF16),
            vmem((4, 16, 2, 16, 256), BF16),
            vmem((128, 1024), BF16),
            vmem((4, 32, 2, 16, 128), BF16),
            vmem((4, 32, 2, 16, 128), BF16),
            dma, dma((2,)), dma((2,)), dma((2,)), dma((2,)), dma((2,)), dma((2,)), dma((2,)), dma((2,)), dma((2, 16)),
            dma, dma((2,)),
            dma((2,)), dma, dma((4,)), dma((4, 4)), dma((4,)), dma((4,)),
        ],
        compiler_params=pltpu.CompilerParams(collective_id=0, has_side_effects=True, vmem_limit_bytes=60 << 20),
    )(source_owner, elemental.reshape(2, 512, 512), perambulators.reshape(2, 16, 2, 16, 512))
    out = pl.pallas_call(
        finish,
        out_shape=jax.ShapeDtypeStruct((2, 16, 32, 512), F32),
        in_specs=[held, held, held],
        out_specs=pl.BlockSpec(memory_space=pltpu.HBM),
        scratch_shapes=[vmem((2, 16, 16, 512), F32), dma((3,))],
        compiler_params=pltpu.CompilerParams(vmem_limit_bytes=12 << 20),
    )(*parts)
    return out.transpose(0, 3, 1, 2)


def solution(mesh):
    in_specs = (P(None, "row", "col", None), P(("row", "col"), None, None, None), P())
    out_specs = P(None, None, "row", "col")
    return jax.shard_map(
        per_device, mesh=mesh, in_specs=in_specs, out_specs=out_specs, check_vma=False
    )
```

```python
import functools

import jax
import jax.numpy as jnp
from jax import lax
from jax.experimental import pallas as pl
from jax.experimental.pallas import tpu as pltpu
from jax.sharding import PartitionSpec as P

MESH = pl.DeviceIdType.MESH
F32 = jnp.float32
BF16 = jnp.bfloat16
NT = (((1,), (1,)), ((), ()))
FAR_FIRST = sorted(
    ((dx, dy) for dx in range(4) for dy in range(4) if dx or dy),
    key=lambda d: -(min(d[0], 4 - d[0]) + min(d[1], 4 - d[1])),
)
ORDER = ((0, (4, 3, 5, 6)), (1, (4, 3, 5, 6)), (1, (2, 7, 1, 0)), (0, (2, 7, 1, 0)))
COL_FAR_FIRST = [(dh, dy, dc) for dh in (1, 0) for dy in (2, 1, 3, 0) for dc in (1, 0) if dh or dy or dc]


def butterfly(arrs, group):
    arrs = list(arrs)
    lane = lax.broadcasted_iota(jnp.int32, arrs[0].shape, 1)
    bit = 1
    while bit < len(arrs):
        shift = group * bit
        high = (lane & shift) != 0
        for a in range(len(arrs)):
            if a & bit:
                continue
            lo, hi = arrs[a], arrs[a | bit]
            arrs[a] = jnp.where(high, pltpu.roll(hi, shift, 1), lo)
            arrs[a | bit] = jnp.where(high, hi, pltpu.roll(lo, 128 - shift, 1))
        bit *= 2
    return arrs


def kernel(
    own_ref, e_ref, p_ref, acc, x3, m3b,
    pb, mine, half, rb0, rb1, cbuf, zb0, zb1, dbuf, zg0, zg1, qbuf, pp, m2, m3a, x1, y1, r1, x2, sb, r2,
    pair_s, pair_r, plane_s, plane_r, zgrp_s, zgrp_r, zall_s, zall_r, gath_s, gath_r, back_s, back_r,
    local_sem, load_sem, col_s, col_r, row_s, row_r,
):
    row = lax.axis_index("row")
    col = lax.axis_index("col")
    x_lo, z = row // 16, row % 16
    core, xy = col % 2, col // 2
    chip = x_lo * 8 + xy
    member, zgroup = z % 4, z // 4
    zhalf, zrest = z // 8, z % 8
    x_hi, y = xy // 4, xy % 4
    rb, zb, zg = (rb0, rb1), (zb0, zb1), (zg0, zg1)
    x = x_hi * 2 + x_lo
    other = (row, xy * 2 + 1 - core)

    def in_plane(dx, dy):
        px, py = (x + dx) % 4, (y + dy) % 4
        to = (px // 2) * 4 + py
        return (px % 2) * 8 + to, ((px % 2) * 16 + z, to * 2 + core)

    barrier = pltpu.get_barrier_semaphore()

    def greet(dev):
        pl.semaphore_signal(barrier, inc=1, device_id=dev, device_id_type=MESH)

    def greet_other(d, _):
        greet((row, d * 2 + 1 - core))
        return 0

    def greet_row(d, _):
        dz = 8 + jnp.where(d % 2 == 0, d // 2, -((d + 1) // 2))
        for px in range(2):
            greet((px * 16 + (z + dz) % 16, col))
        return 0

    for step in FAR_FIRST:
        greet(in_plane(*step)[1])
    lax.fori_loop(0, 8, greet_other, 0)
    lax.fori_loop(0, 15, greet_row, 0)

    for t in range(2):
        pltpu.make_async_copy(p_ref.at[core, :, t], mine.at[t], local_sem.at[t]).start()
    for r in range(2):
        pltpu.make_async_copy(e_ref.at[r], x1.at[:, pl.ds(r * 512, 512)], load_sem).start()
    pl.semaphore_wait(barrier, 53)

    def send(src, dst, ssem, rsem, dev):
        pltpu.make_async_remote_copy(
            src_ref=src, dst_ref=dst, send_sem=ssem, recv_sem=rsem,
            device_id=dev, device_id_type=MESH,
        ).start()

    def wait_bytes(ref, sem):
        pltpu.make_async_copy(ref, ref, sem).wait()

    owner = own_ref[0]
    owner_row, owner_col = lax.div(owner, 16), lax.rem(owner, 16)
    from_me = lax.rem(owner_col, 2) == core
    owner_chip = lax.div(owner_row, 16) * 8 + lax.div(owner_col, 2)
    owner_z = lax.rem(owner_row, 16)

    def lanes128(n):
        return pl.ds(pl.multiple_of(n * 128, 128), 128)

    for t in range(2):
        send(p_ref.at[1 - core, :, t], pb.at[t], pair_s, pair_r.at[t], other)

    for t in range(2):
        wait_bytes(mine.at[t], local_sem.at[t])
        wait_bytes(pb.at[t], pair_r.at[t])

        def pick(n, _, t=t):
            half[t, n] = jnp.where(from_me, mine[t, n], pb[t, n])
            return 0

        lax.fori_loop(0, 16, pick, 0)
        for step in FAR_FIRST:
            c, to = in_plane(*step)
            send(half.at[t, c], rb[t].at[chip], plane_s.at[t], plane_r.at[t], to)
        pltpu.make_async_copy(half.at[t, chip], rb[t].at[chip], plane_r.at[t]).start()

    for t in range(2):
        wait_bytes(rb[t], plane_r.at[t])
        cbuf[t] = rb[t][owner_chip]

        def scatter_z(d, _, t=t):
            to = (x_lo * 16 + zgroup * 4 + (member + d) % 4, col)
            send(cbuf.at[t, :, lanes128((member + d) % 4)], zb[t].at[member], zgrp_s.at[t], zgrp_r.at[t], to)
            return 0

        lax.fori_loop(1, 4, scatter_z, 0)
        pltpu.make_async_copy(cbuf.at[t, :, lanes128(member)], zb[t].at[member], zgrp_r.at[t]).start()
    for t in range(2):
        wait_bytes(zb[t], zgrp_r.at[t])
        dbuf[t] = zb[t][lax.rem(owner_z, 4)]

        def gather_z(d, _, t=t):
            dz = 8 + jnp.where(d % 2 == 0, d // 2, -((d + 1) // 2))
            send(dbuf.at[t], zg[t].at[z], zall_s.at[t], zall_r.at[t], (x_lo * 16 + (z + dz) % 16, col))
            return 0

        lax.fori_loop(0, 15, gather_z, 0)
        pltpu.make_async_copy(dbuf.at[t], zg[t].at[z], zall_r.at[t]).start()

    for t in range(2):
        wait_bytes(zg[t], zall_r.at[t])
        for m in range(4):
            qbuf[t, :, m * 128 : (m + 1) * 128] = zg[t][lax.div(owner_z, 4) * 4 + m]
        for step in FAR_FIRST:
            send(qbuf.at[t], pp.at[core, t, chip], gath_s.at[t], gath_r.at[t, chip], in_plane(*step)[1])
        pltpu.make_async_copy(qbuf.at[t], pp.at[core, t, chip], gath_r.at[t, chip]).start()

    def gather_pair(t):
        for step in ((0, 0), *FAR_FIRST):
            c = in_plane(*step)[0]
            part = pp.at[core, t, c]
            wait_bytes(part, gath_r.at[t, c])
            send(part, part, back_s, back_r.at[t], other)
        wait_bytes(pb.at[t], back_r.at[t])

        def build(n, _):
            re, im = pp[0, t, n], pp[1, t, n]
            m2[0, n, t, :, 0:512] = re
            m2[0, n, t, :, 512:1024] = -im
            m2[1, n, t, :, 0:512] = im
            m2[1, n, t, :, 512:1024] = re
            return 0

        lax.fori_loop(0, 16, build, 0)

    def contract_k(q):
        h, ch = q // 2, q % 2
        for s in range(2):
            y = lax.dot_general(
                m2[s, :, ch].reshape(256, 1024), x1[h * 256 : (h + 1) * 256, :], NT, preferred_element_type=F32
            )
            y1[q, s] = y.astype(BF16)

    def exchange_col(q):
        for dh, dy, dc in COL_FAR_FIRST:
            c = (((x_hi + dh) % 2) * 4 + (y + dy) % 4) * 2 + (core + dc) % 2
            rows = pl.ds(pl.multiple_of(c * 16, 16), 16)
            send(y1.at[q, :, rows, :], r1.at[q, col], col_s.at[q], col_r.at[q, col // 4], (row, c))
        rows = pl.ds(pl.multiple_of(col * 16, 16), 16)
        pltpu.make_async_copy(y1.at[q, :, rows, :], r1.at[q, col], col_r.at[q, col // 4]).start()

    def contract_j(q):
        def swap_in(n, _):
            chi = (col // 4 + n) % 4
            wait_bytes(r1.at[q, pl.ds(chi * 4, 4)], col_r.at[q, chi])
            for r in range(2):
                for ib in range(2):
                    got = [r1[q, chi * 4 + k, r, :, ib * 128 : (ib + 1) * 128] for k in range(4)]
                    for k, v in enumerate(butterfly(got, 32)):
                        x2[(ib * 4 + k) * 16 : (ib * 4 + k + 1) * 16, lanes128(r * 4 + chi)] = v
            return 0

        lax.fori_loop(0, 4, swap_in, 0)

        for dx, steps in ORDER:
            to_x = (x_lo + dx) % 2
            pairs = [(z // 2 + step) % 8 for step in steps]
            rhs = jnp.concatenate([m2[:, to_x * 8 + p].reshape(2, 32, 1024) for p in pairs], axis=1)
            v = lax.dot_general(x2[...], rhs.reshape(256, 1024), NT, preferred_element_type=F32).astype(BF16)
            for s in range(2):
                got = [v[k * 16 : (k + 1) * 16, s * 128 : (s + 1) * 128] for k in range(8)]
                for k, w in enumerate(butterfly(got, 16)):
                    sb[q, to_x * 16 + pairs[k // 2] * 2 + k % 2, s, :, :] = w

            def scatter_row(n, _):
                k = n // 2
                step = jnp.where(k == 0, steps[0], jnp.where(k == 1, steps[1], jnp.where(k == 2, steps[2], steps[3])))
                to = to_x * 16 + ((z // 2 + step) % 8) * 2 + (z + 1 + n) % 2
                send(sb.at[q, to], r2.at[q, row], row_s.at[q], row_r.at[q, x_lo], (to, col))
                return 0

            lax.fori_loop(0, 8 if dx or steps[3] else 7, scatter_row, 0)
        pltpu.make_async_copy(sb.at[q, row], r2.at[q, row], row_r.at[q, x_lo]).start()

    gather_pair(0)
    wait_bytes(x1, load_sem)
    contract_k(0)
    exchange_col(0)
    gather_pair(1)
    contract_k(1)
    exchange_col(1)
    contract_k(2)
    contract_k(3)
    contract_j(0)
    exchange_col(2)
    contract_j(1)
    exchange_col(3)
    contract_j(2)
    contract_j(3)

    a = lax.broadcasted_iota(jnp.int32, (256, 128), 0)
    b = lax.broadcasted_iota(jnp.int32, (256, 128), 1)
    for h in range(2):
        perm = (a == (b % 16) * 16 + h * 8 + b // 16).astype(F32).astype(BF16)

        m3 = (m3a, m3b)[h]

        def permute(n, _, m3=m3, perm=perm):
            block = m2[n // 2, pl.ds((n % 2) * 8, 8)].reshape(256, 1024)
            rows = pl.ds(pl.multiple_of(n * 256, 256), 256)
            for k in range(4):
                v = jnp.dot(block[:, k * 256 : (k + 1) * 256], perm, preferred_element_type=F32)
                m3[rows, k * 128 : (k + 1) * 128] = v.astype(BF16)
            return 0

        lax.fori_loop(0, 4, permute, 0)

    for q in range(4):
        ch = q % 2
        for dx in (1, 0):
            from_x = (x_lo + dx) % 2
            wait_bytes(r2.at[q, pl.ds(from_x * 16, 16)], row_r.at[q, from_x])

            def swap_out(r, _, q=q, from_x=from_x):
                got = [r2[q, from_x * 16 + k, r, :, :] for k in range(16)]
                for k, v in enumerate(butterfly(got, 1)):
                    x3[k * 16 : (k + 1) * 16, lanes128(r * 2 + from_x)] = v
                return 0

            lax.fori_loop(0, 2, swap_out, 0)
        if q == 3:
            break
        m3 = (m3a, m3b)[q // 2]

        def contract_i(n, _, q=q, ch=ch, m3=m3):
            rows = pl.ds(pl.multiple_of(n * 256, 256), 256)
            lanes = pl.ds(pl.multiple_of((n % 2) * 256, 256), 256)
            v = lax.dot_general(x3[...], m3[rows, :], NT, preferred_element_type=F32).reshape(16, 16, 256)
            if q < 2:
                acc[ch, n // 2, :, :, lanes] = v
            else:
                acc[ch, n // 2, :, :, lanes] += v
            return 0

        lax.fori_loop(0, 4, contract_i, 0)

    wait_bytes(pb, pair_s)
    wait_bytes(pb, back_s)
    for t in range(2):
        wait_bytes(rb[t].at[pl.ds(0, 15)], plane_s.at[t])
        wait_bytes(zb[t].at[pl.ds(0, 3)], zgrp_s.at[t])
        wait_bytes(zg[t].at[pl.ds(0, 15)], zall_s.at[t])
        wait_bytes(rb[t].at[pl.ds(0, 15)], gath_s.at[t])
    for q in range(4):
        wait_bytes(r1.at[q, pl.ds(0, 15)], col_s.at[q])
        wait_bytes(r2.at[q, pl.ds(0, 31)], row_s.at[q])


def finish(acc, x3, m3, out_ref, last, sem):
    done = pltpu.make_async_copy(acc.at[0], out_ref.at[:, :, pl.ds(0, 16), :], sem.at[2])
    done.start()
    copies = []
    for s in range(2):
        for lane in range(0, 512, 256):
            v = lax.dot_general(
                x3[...], m3[s * 512 + lane : s * 512 + lane + 256, :], NT, preferred_element_type=F32
            )
            last[s, :, :, lane : lane + 256] = acc[1, s, :, :, lane : lane + 256] + v.reshape(16, 16, 256)
        copies.append(pltpu.make_async_copy(last.at[s], out_ref.at[s, :, pl.ds(16, 16), :], sem.at[s]))
        copies[-1].start()
    for copy in (done, *copies):
        copy.wait()


def per_device(elemental, perambulators, source_owner):
    dma = pltpu.SemaphoreType.DMA
    vmem = pltpu.VMEM
    held = pl.BlockSpec(memory_space=pltpu.VMEM)
    parts = pl.pallas_call(
        kernel,
        out_shape=(vmem((2, 2, 16, 16, 512), F32), vmem((256, 512), BF16), vmem((1024, 512), BF16)),
        in_specs=[
            pl.BlockSpec(memory_space=pltpu.SMEM),
            pl.BlockSpec(memory_space=pltpu.HBM),
            pl.BlockSpec(memory_space=pltpu.HBM),
        ],
        out_specs=(held, held, held),
        scratch_shapes=[
            vmem((2, 16, 16, 512), BF16),
            vmem((2, 16, 16, 512), BF16),
            vmem((2, 16, 16, 512), BF16),
            vmem((16, 16, 512), BF16),
            vmem((16, 16, 512), BF16),
            vmem((2, 16, 512), BF16),
            vmem((4, 16, 128), BF16),
            vmem((4, 16, 128), BF16),
            vmem((2, 16, 128), BF16),
            vmem((16, 16, 128), BF16),
            vmem((16, 16, 128), BF16),
            vmem((2, 16, 512), BF16),
            vmem((2, 2, 16, 16, 512), BF16),
            vmem((2, 16, 2, 16, 1024), BF16),
            vmem((1024, 512), BF16),
            vmem((512, 1024), BF16),
            vmem((4, 2, 256, 256), BF16),
            vmem((4, 16, 2, 16, 256), BF16),
            vmem((128, 1024), BF16),
            vmem((4, 32, 2, 16, 128), BF16),
            vmem((4, 32, 2, 16, 128), BF16),
            dma, dma((2,)), dma((2,)), dma((2,)), dma((2,)), dma((2,)), dma((2,)), dma((2,)), dma((2,)), dma((2, 16)),
            dma, dma((2,)),
            dma((2,)), dma, dma((4,)), dma((4, 4)), dma((4,)), dma((4, 2)),
        ],
        compiler_params=pltpu.CompilerParams(collective_id=0, has_side_effects=True, vmem_limit_bytes=60 << 20),
    )(source_owner, elemental.reshape(2, 512, 512), perambulators.reshape(2, 16, 2, 16, 512))
    out = pl.pallas_call(
        finish,
        out_shape=jax.ShapeDtypeStruct((2, 16, 32, 512), F32),
        in_specs=[held, held, held],
        out_specs=pl.BlockSpec(memory_space=pltpu.HBM),
        scratch_shapes=[vmem((2, 16, 16, 512), F32), dma((3,))],
        compiler_params=pltpu.CompilerParams(vmem_limit_bytes=12 << 20),
    )(*parts)
    return out.transpose(0, 3, 1, 2)


def solution(mesh):
    in_specs = (P(None, "row", "col", None), P(("row", "col"), None, None, None), P())
    out_specs = P(None, None, "row", "col")
    return jax.shard_map(
        per_device, mesh=mesh, in_specs=in_specs, out_specs=out_specs, check_vma=False
    )
```

```python
import functools

import jax
import jax.numpy as jnp
from jax import lax
from jax.experimental import pallas as pl
from jax.experimental.pallas import tpu as pltpu
from jax.sharding import PartitionSpec as P

MESH = pl.DeviceIdType.MESH
F32 = jnp.float32
BF16 = jnp.bfloat16
NT = (((1,), (1,)), ((), ()))
FAR_FIRST = sorted(
    ((dx, dy) for dx in range(4) for dy in range(4) if dx or dy),
    key=lambda d: -(min(d[0], 4 - d[0]) + min(d[1], 4 - d[1])),
)
ORDER = ((0, (4, 3, 5, 6)), (1, (4, 3, 5, 6)), (1, (2, 7, 1, 0)), (0, (2, 7, 1, 0)))
COL_FAR_FIRST = [(dh, dy, dc) for dh in (1, 0) for dy in (2, 1, 3, 0) for dc in (1, 0) if dh or dy or dc]


def butterfly(arrs, group):
    arrs = list(arrs)
    lane = lax.broadcasted_iota(jnp.int32, arrs[0].shape, 1)
    bit = 1
    while bit < len(arrs):
        shift = group * bit
        high = (lane & shift) != 0
        for a in range(len(arrs)):
            if a & bit:
                continue
            lo, hi = arrs[a], arrs[a | bit]
            arrs[a] = jnp.where(high, pltpu.roll(hi, shift, 1), lo)
            arrs[a | bit] = jnp.where(high, hi, pltpu.roll(lo, 128 - shift, 1))
        bit *= 2
    return arrs


def kernel(
    own_ref, e_ref, p_ref, acc, x3, m3b,
    pb, mine, half, rb0, rb1, cbuf, zb0, zb1, dbuf, zg0, zg1, qbuf, pp, m2, m3a, x1, y1, r1, x2, sb, r2,
    pair_s, pair_r, plane_s, plane_r, zgrp_s, zgrp_r, zall_s, zall_r, gath_s, gath_r, back_s, back_r,
    local_sem, load_sem, col_s, col_r, row_s, row_r,
):
    row = lax.axis_index("row")
    col = lax.axis_index("col")
    x_lo, z = row // 16, row % 16
    core, xy = col % 2, col // 2
    chip = x_lo * 8 + xy
    member, zgroup = z % 4, z // 4
    zhalf, zrest = z // 8, z % 8
    x_hi, y = xy // 4, xy % 4
    rb, zb, zg = (rb0, rb1), (zb0, zb1), (zg0, zg1)
    x = x_hi * 2 + x_lo
    other = (row, xy * 2 + 1 - core)

    def in_plane(dx, dy):
        px, py = (x + dx) % 4, (y + dy) % 4
        to = (px // 2) * 4 + py
        return (px % 2) * 8 + to, ((px % 2) * 16 + z, to * 2 + core)

    barrier = pltpu.get_barrier_semaphore()

    def greet(dev):
        pl.semaphore_signal(barrier, inc=1, device_id=dev, device_id_type=MESH)

    def greet_other(d, _):
        greet((row, d * 2 + 1 - core))
        return 0

    def greet_row(d, _):
        dz = 8 + jnp.where(d % 2 == 0, d // 2, -((d + 1) // 2))
        for px in range(2):
            greet((px * 16 + (z + dz) % 16, col))
        return 0

    lax.fori_loop(0, 15, greet_row, 0)
    for step in FAR_FIRST:
        greet(in_plane(*step)[1])
    lax.fori_loop(0, 8, greet_other, 0)

    for t in range(2):
        pltpu.make_async_copy(p_ref.at[core, :, t], mine.at[t], local_sem.at[t]).start()
    for r in range(2):
        pltpu.make_async_copy(e_ref.at[r], x1.at[:, pl.ds(r * 512, 512)], load_sem).start()
    pl.semaphore_wait(barrier, 53)

    def send(src, dst, ssem, rsem, dev):
        pltpu.make_async_remote_copy(
            src_ref=src, dst_ref=dst, send_sem=ssem, recv_sem=rsem,
            device_id=dev, device_id_type=MESH,
        ).start()

    def wait_bytes(ref, sem):
        pltpu.make_async_copy(ref, ref, sem).wait()

    owner = own_ref[0]
    owner_row, owner_col = lax.div(owner, 16), lax.rem(owner, 16)
    from_me = lax.rem(owner_col, 2) == core
    owner_chip = lax.div(owner_row, 16) * 8 + lax.div(owner_col, 2)
    owner_z = lax.rem(owner_row, 16)

    def lanes128(n):
        return pl.ds(pl.multiple_of(n * 128, 128), 128)

    for t in range(2):
        send(p_ref.at[1 - core, :, t], pb.at[t], pair_s, pair_r.at[t], other)

    for t in range(2):
        wait_bytes(mine.at[t], local_sem.at[t])
        wait_bytes(pb.at[t], pair_r.at[t])

        def pick(n, _, t=t):
            half[t, n] = jnp.where(from_me, mine[t, n], pb[t, n])
            return 0

        lax.fori_loop(0, 16, pick, 0)
        for step in FAR_FIRST:
            c, to = in_plane(*step)
            send(half.at[t, c], rb[t].at[chip], plane_s.at[t], plane_r.at[t], to)
        pltpu.make_async_copy(half.at[t, chip], rb[t].at[chip], plane_r.at[t]).start()

    for t in range(2):
        wait_bytes(rb[t], plane_r.at[t])
        cbuf[t] = rb[t][owner_chip]

        def scatter_z(d, _, t=t):
            to = (x_lo * 16 + zgroup * 4 + (member + d) % 4, col)
            send(cbuf.at[t, :, lanes128((member + d) % 4)], zb[t].at[member], zgrp_s.at[t], zgrp_r.at[t], to)
            return 0

        lax.fori_loop(1, 4, scatter_z, 0)
        pltpu.make_async_copy(cbuf.at[t, :, lanes128(member)], zb[t].at[member], zgrp_r.at[t]).start()
    for t in range(2):
        wait_bytes(zb[t], zgrp_r.at[t])
        dbuf[t] = zb[t][lax.rem(owner_z, 4)]

        def gather_z(d, _, t=t):
            dz = 8 + jnp.where(d % 2 == 0, d // 2, -((d + 1) // 2))
            send(dbuf.at[t], zg[t].at[z], zall_s.at[t], zall_r.at[t], (x_lo * 16 + (z + dz) % 16, col))
            return 0

        lax.fori_loop(0, 15, gather_z, 0)
        pltpu.make_async_copy(dbuf.at[t], zg[t].at[z], zall_r.at[t]).start()

    for t in range(2):
        wait_bytes(zg[t], zall_r.at[t])
        for m in range(4):
            qbuf[t, :, m * 128 : (m + 1) * 128] = zg[t][lax.div(owner_z, 4) * 4 + m]
        for step in FAR_FIRST:
            send(qbuf.at[t], pp.at[core, t, chip], gath_s.at[t], gath_r.at[t, chip], in_plane(*step)[1])
        pltpu.make_async_copy(qbuf.at[t], pp.at[core, t, chip], gath_r.at[t, chip]).start()

    def gather_pair(t):
        for step in ((0, 0), *FAR_FIRST):
            c = in_plane(*step)[0]
            part = pp.at[core, t, c]
            wait_bytes(part, gath_r.at[t, c])
            send(part, part, back_s, back_r.at[t], other)
        wait_bytes(pb.at[t], back_r.at[t])

        def build(n, _):
            re, im = pp[0, t, n], pp[1, t, n]
            m2[0, n, t, :, 0:512] = re
            m2[0, n, t, :, 512:1024] = -im
            m2[1, n, t, :, 0:512] = im
            m2[1, n, t, :, 512:1024] = re
            return 0

        lax.fori_loop(0, 16, build, 0)

    def contract_k(q):
        h, ch = q // 2, q % 2
        for s in range(2):
            y = lax.dot_general(
                m2[s, :, ch].reshape(256, 1024), x1[h * 256 : (h + 1) * 256, :], NT, preferred_element_type=F32
            )
            y1[q, s] = y.astype(BF16)

    def exchange_col(q):
        for dh, dy, dc in COL_FAR_FIRST:
            c = (((x_hi + dh) % 2) * 4 + (y + dy) % 4) * 2 + (core + dc) % 2
            rows = pl.ds(pl.multiple_of(c * 16, 16), 16)
            send(y1.at[q, :, rows, :], r1.at[q, col], col_s.at[q], col_r.at[q, col // 4], (row, c))
        rows = pl.ds(pl.multiple_of(col * 16, 16), 16)
        pltpu.make_async_copy(y1.at[q, :, rows, :], r1.at[q, col], col_r.at[q, col // 4]).start()

    def contract_j(q):
        def swap_in(n, _):
            chi = (col // 4 + n) % 4
            wait_bytes(r1.at[q, pl.ds(chi * 4, 4)], col_r.at[q, chi])
            for r in range(2):
                for ib in range(2):
                    got = [r1[q, chi * 4 + k, r, :, ib * 128 : (ib + 1) * 128] for k in range(4)]
                    for k, v in enumerate(butterfly(got, 32)):
                        x2[(ib * 4 + k) * 16 : (ib * 4 + k + 1) * 16, lanes128(r * 4 + chi)] = v
            return 0

        lax.fori_loop(0, 4, swap_in, 0)

        for dx, steps in ORDER:
            to_x = (x_lo + dx) % 2
            pairs = [(z // 2 + step) % 8 for step in steps]
            rhs = jnp.concatenate([m2[:, to_x * 8 + p].reshape(2, 32, 1024) for p in pairs], axis=1)
            v = lax.dot_general(x2[...], rhs.reshape(256, 1024), NT, preferred_element_type=F32).astype(BF16)
            for s in range(2):
                got = [v[k * 16 : (k + 1) * 16, s * 128 : (s + 1) * 128] for k in range(8)]
                for k, w in enumerate(butterfly(got, 16)):
                    sb[q, to_x * 16 + pairs[k // 2] * 2 + k % 2, s, :, :] = w

            def scatter_row(n, _):
                k = n // 2
                step = jnp.where(k == 0, steps[0], jnp.where(k == 1, steps[1], jnp.where(k == 2, steps[2], steps[3])))
                to = to_x * 16 + ((z // 2 + step) % 8) * 2 + (z + 1 + n) % 2
                send(sb.at[q, to], r2.at[q, row], row_s.at[q], row_r.at[q, x_lo], (to, col))
                return 0

            lax.fori_loop(0, 8 if dx or steps[3] else 7, scatter_row, 0)
        pltpu.make_async_copy(sb.at[q, row], r2.at[q, row], row_r.at[q, x_lo]).start()

    gather_pair(0)
    wait_bytes(x1, load_sem)
    contract_k(0)
    exchange_col(0)
    gather_pair(1)
    contract_k(1)
    exchange_col(1)
    contract_k(2)
    contract_k(3)
    contract_j(0)
    exchange_col(2)
    contract_j(1)
    exchange_col(3)
    contract_j(2)
    contract_j(3)

    a = lax.broadcasted_iota(jnp.int32, (256, 128), 0)
    b = lax.broadcasted_iota(jnp.int32, (256, 128), 1)
    for h in range(2):
        perm = (a == (b % 16) * 16 + h * 8 + b // 16).astype(F32).astype(BF16)

        m3 = (m3a, m3b)[h]

        def permute(n, _, m3=m3, perm=perm):
            block = m2[n // 2, pl.ds((n % 2) * 8, 8)].reshape(256, 1024)
            rows = pl.ds(pl.multiple_of(n * 256, 256), 256)
            for k in range(4):
                v = jnp.dot(block[:, k * 256 : (k + 1) * 256], perm, preferred_element_type=F32)
                m3[rows, k * 128 : (k + 1) * 128] = v.astype(BF16)
            return 0

        lax.fori_loop(0, 4, permute, 0)

    for q in range(4):
        ch = q % 2
        for dx in (1, 0):
            from_x = (x_lo + dx) % 2
            wait_bytes(r2.at[q, pl.ds(from_x * 16, 16)], row_r.at[q, from_x])

            def swap_out(r, _, q=q, from_x=from_x):
                got = [r2[q, from_x * 16 + k, r, :, :] for k in range(16)]
                for k, v in enumerate(butterfly(got, 1)):
                    x3[k * 16 : (k + 1) * 16, lanes128(r * 2 + from_x)] = v
                return 0

            lax.fori_loop(0, 2, swap_out, 0)
        if q == 3:
            break
        m3 = (m3a, m3b)[q // 2]

        def contract_i(n, _, q=q, ch=ch, m3=m3):
            rows = pl.ds(pl.multiple_of(n * 256, 256), 256)
            lanes = pl.ds(pl.multiple_of((n % 2) * 256, 256), 256)
            v = lax.dot_general(x3[...], m3[rows, :], NT, preferred_element_type=F32).reshape(16, 16, 256)
            if q < 2:
                acc[ch, n // 2, :, :, lanes] = v
            else:
                acc[ch, n // 2, :, :, lanes] += v
            return 0

        lax.fori_loop(0, 4, contract_i, 0)

    wait_bytes(pb, pair_s)
    wait_bytes(pb, back_s)
    for t in range(2):
        wait_bytes(rb[t].at[pl.ds(0, 15)], plane_s.at[t])
        wait_bytes(zb[t].at[pl.ds(0, 3)], zgrp_s.at[t])
        wait_bytes(zg[t].at[pl.ds(0, 15)], zall_s.at[t])
        wait_bytes(rb[t].at[pl.ds(0, 15)], gath_s.at[t])
    for q in range(4):
        wait_bytes(r1.at[q, pl.ds(0, 15)], col_s.at[q])
        wait_bytes(r2.at[q, pl.ds(0, 31)], row_s.at[q])


def finish(acc, x3, m3, out_ref, last, sem):
    done = pltpu.make_async_copy(acc.at[0], out_ref.at[:, :, pl.ds(0, 16), :], sem.at[2])
    done.start()
    copies = []
    for s in range(2):
        for lane in range(0, 512, 256):
            v = lax.dot_general(
                x3[...], m3[s * 512 + lane : s * 512 + lane + 256, :], NT, preferred_element_type=F32
            )
            last[s, :, :, lane : lane + 256] = acc[1, s, :, :, lane : lane + 256] + v.reshape(16, 16, 256)
        copies.append(pltpu.make_async_copy(last.at[s], out_ref.at[s, :, pl.ds(16, 16), :], sem.at[s]))
        copies[-1].start()
    for copy in (done, *copies):
        copy.wait()


def per_device(elemental, perambulators, source_owner):
    dma = pltpu.SemaphoreType.DMA
    vmem = pltpu.VMEM
    held = pl.BlockSpec(memory_space=pltpu.VMEM)
    parts = pl.pallas_call(
        kernel,
        out_shape=(vmem((2, 2, 16, 16, 512), F32), vmem((256, 512), BF16), vmem((1024, 512), BF16)),
        in_specs=[
            pl.BlockSpec(memory_space=pltpu.SMEM),
            pl.BlockSpec(memory_space=pltpu.HBM),
            pl.BlockSpec(memory_space=pltpu.HBM),
        ],
        out_specs=(held, held, held),
        scratch_shapes=[
            vmem((2, 16, 16, 512), BF16),
            vmem((2, 16, 16, 512), BF16),
            vmem((2, 16, 16, 512), BF16),
            vmem((16, 16, 512), BF16),
            vmem((16, 16, 512), BF16),
            vmem((2, 16, 512), BF16),
            vmem((4, 16, 128), BF16),
            vmem((4, 16, 128), BF16),
            vmem((2, 16, 128), BF16),
            vmem((16, 16, 128), BF16),
            vmem((16, 16, 128), BF16),
            vmem((2, 16, 512), BF16),
            vmem((2, 2, 16, 16, 512), BF16),
            vmem((2, 16, 2, 16, 1024), BF16),
            vmem((1024, 512), BF16),
            vmem((512, 1024), BF16),
            vmem((4, 2, 256, 256), BF16),
            vmem((4, 16, 2, 16, 256), BF16),
            vmem((128, 1024), BF16),
            vmem((4, 32, 2, 16, 128), BF16),
            vmem((4, 32, 2, 16, 128), BF16),
            dma, dma((2,)), dma((2,)), dma((2,)), dma((2,)), dma((2,)), dma((2,)), dma((2,)), dma((2,)), dma((2, 16)),
            dma, dma((2,)),
            dma((2,)), dma, dma((4,)), dma((4, 4)), dma((4,)), dma((4, 2)),
        ],
        compiler_params=pltpu.CompilerParams(collective_id=0, has_side_effects=True, vmem_limit_bytes=60 << 20),
    )(source_owner, elemental.reshape(2, 512, 512), perambulators.reshape(2, 16, 2, 16, 512))
    out = pl.pallas_call(
        finish,
        out_shape=jax.ShapeDtypeStruct((2, 16, 32, 512), F32),
        in_specs=[held, held, held],
        out_specs=pl.BlockSpec(memory_space=pltpu.HBM),
        scratch_shapes=[vmem((2, 16, 16, 512), F32), dma((3,))],
        compiler_params=pltpu.CompilerParams(vmem_limit_bytes=12 << 20),
    )(*parts)
    return out.transpose(0, 3, 1, 2)


def solution(mesh):
    in_specs = (P(None, "row", "col", None), P(("row", "col"), None, None, None), P())
    out_specs = P(None, None, "row", "col")
    return jax.shard_map(
        per_device, mesh=mesh, in_specs=in_specs, out_specs=out_specs, check_vma=False
    )
```
